32 devices in a mesh: feat: 16 (over z, y, core), width: 2 (over x).
Axes of the slice: x: 2, y: 2, z: 4, core: 2. Of those that a mesh axis runs over, the one named last changes fastest.
Arguments:
- dec_rows: bfloat16 [32768, 8192], P('feat', 'width'), may hold values from -6 to 6
- enc_rows: bfloat16 [32768, 8192], P('feat', 'width'), may hold values from -0.0625 to 0.0625
- src_act: float32 [4096], replicated, may hold values from 0.25 to 4
- src_slots: int32 [256, 12], P('feat'), may hold values from 0 to 15, as said below
- counts: int32 [256], P('feat'), may hold values from 1 to 12, as said below
- used_tiles: int32 [8, 16], replicated, may hold values from 0 to 31, as said below
Outputs:
- edges: bfloat16 [256, 12, 128, 128], P('feat', None, 'width')
The draws below stay inside these ranges and needn't reach their ends.
Inputs may be any that keep to these rules, and one draw needn't show every extreme that they name: `src_slots`: the slot numbers in one row are distinct. Slots 0 to counts - 1 of a row are live; some row has all 12 live. `used_tiles`: each row rises strictly; of each aligned run of 16 tile numbers exactly half are listed.
All inputs are finite; a program needn't handle non-finite values.
Results may differ from the reference program's by a relative error of at most 0.001.
Values may be sent and summed in bfloat16 or wider, within the bound.
A program may use at most 192 MiB of HBM per device.

```python
import math
import jax
import jax.numpy as jnp
from jax import lax

D = 8192
LAYERS = 8
SRC = 4096
TGT = 4096
TILE = 128
MAXS = 12
GROUP = 2
S_TILES = 32
T_TILES = 32
USED = 16


def draw_src_slots(key, part):
    keys = jax.random.split(jax.random.fold_in(key, 11), LAYERS * T_TILES)
    picked = jax.vmap(lambda single: jax.random.permutation(single, USED)[:MAXS])(keys)
    return picked.astype(jnp.int32)


def draw_counts(key, part):
    first, second, third = jax.random.split(jax.random.fold_in(key, 23), 3)
    total = LAYERS * T_TILES
    heavy = jax.random.randint(first, (total,), 0, 4)
    light = jax.random.randint(second, (total,), 1, MAXS // 2 + 1)
    values = jnp.where(heavy == 0, MAXS, light)
    chosen = jax.random.randint(third, (), 0, total)
    values = values.at[chosen].set(MAXS)
    return values.astype(jnp.int32)


def draw_used_tiles(key, part):
    per_member = S_TILES // GROUP
    take_count = USED // GROUP
    keys = jax.random.split(jax.random.fold_in(key, 37), LAYERS * GROUP)
    picked = jax.vmap(lambda single: jnp.sort(jax.random.permutation(single, per_member)[:take_count]))(keys)
    offsets = jnp.arange(LAYERS * GROUP, dtype=jnp.int32) % GROUP * per_member
    return (picked + offsets[:, None]).reshape(LAYERS, USED).astype(jnp.int32)


def levels(rng, extent, pieces, smallest, largest):
    gain, own = 1.0, jax.random.fold_in(rng, 6)
    for position, parts in pieces:
        steps = jnp.exp(jax.random.uniform(jax.random.fold_in(own, position), (parts,), jnp.float32, smallest / len(pieces), largest / len(pieces)))
        gain = gain * jnp.repeat(steps, extent[position] // parts).reshape([-1 if axis == position else 1 for axis in range(len(extent))])
    return gain


def normal_values(own_key, extent, spread, reach, pieces=(), kind=jnp.bfloat16):
    entries = spread * jax.random.normal(own_key, extent, jnp.float32)
    if pieces:
        entries = entries * levels(own_key, extent, pieces, -0.22, 0.18)
    return jnp.clip(entries, -reach, reach).astype(kind)


def setup_inputs(seed: int = 0) -> dict:
    key_list = jax.random.split(jax.random.key(seed), 7)
    dec_rows = normal_values(key_list[0], (LAYERS * SRC, D), 1.0, 6.0, ((0, 16), (1, 2)))
    enc_rows = normal_values(key_list[1], (LAYERS * TGT, D), D ** -0.5, 0.0625, ((0, 16), (1, 2)))
    src_act = jnp.clip(jnp.exp(jax.random.uniform(key_list[2], (SRC,), jnp.float32, math.log(0.25), math.log(4.0))), 0.25, 4.0)
    src_slots = draw_src_slots(jax.random.fold_in(key_list[6], 71), 0)
    counts = draw_counts(jax.random.fold_in(key_list[6], 71), 0)
    used_tiles = draw_used_tiles(jax.random.fold_in(key_list[6], 71), 0)
    return dict(dec_rows=dec_rows, enc_rows=enc_rows, src_act=src_act, src_slots=src_slots, counts=counts, used_tiles=used_tiles)


def reference(dec_rows, enc_rows, src_act, src_slots, counts, used_tiles):
    source_tiles = SRC // TILE
    target_tiles = TGT // TILE
    dec_tiles = dec_rows.reshape(LAYERS * source_tiles, TILE, D)
    act_tiles = src_act.reshape(source_tiles, TILE)

    def one_tile(index):
        layer_at = index // target_tiles
        tile_at = index % target_tiles
        start = (layer_at * TGT + tile_at * TILE).astype(jnp.int32)
        target = lax.dynamic_slice_in_dim(enc_rows, start, TILE, 0)
        tile_ids = used_tiles[layer_at][src_slots[index]].astype(jnp.int32)
        src_rows = dec_tiles[(layer_at * source_tiles + tile_ids).astype(jnp.int32)].reshape(MAXS * TILE, D)
        products = lax.dot_general(src_rows, target, (((1,), (1,)), ((), ())), preferred_element_type=jnp.float32)
        products = products.reshape(MAXS, TILE, TILE)
        scaled = products * act_tiles[tile_ids][:, :, None]
        is_live = jnp.arange(MAXS, dtype=jnp.int32) < counts[index]
        return jnp.where(is_live[:, None, None], scaled, jnp.zeros_like(scaled)).astype(jnp.bfloat16)

    return lax.map(one_tile, jnp.arange(LAYERS * target_tiles, dtype=jnp.int32))
```

```python
import functools

import jax
import jax.numpy as jnp
from jax import lax
from jax.experimental import pallas as pl
from jax.experimental.pallas import tpu as pltpu
from jax.sharding import PartitionSpec as P

CHUNK = 8
TOP = 32767.0
MESH = pl.DeviceIdType.MESH


def take_kernel(ids, src, dst):
    dst[...] = src[...]


def take_tiles(tiles, ids):
    count = ids.shape[0]
    block = (1,) + tiles.shape[1:]
    return pl.pallas_call(
        take_kernel,
        grid_spec=pltpu.PrefetchScalarGridSpec(
            num_scalar_prefetch=1,
            grid=(count,),
            in_specs=[pl.BlockSpec(block, lambda i, ids: (ids[i], 0, 0))],
            out_specs=pl.BlockSpec(block, lambda i, ids: (i, 0, 0)),
        ),
        out_shape=jax.ShapeDtypeStruct((count,) + tiles.shape[1:], tiles.dtype),
        name="take_tiles",
    )(ids, tiles)


def edge_kernel(
    items, group, width,
    item_tile, item_src, act, own, enc, out,
    table, targets, product, kept, sent, sent_scale, got, got_scale,
    load_sem, own_sem, group_send, group_recv, data_send, data_recv, scale_send, scale_recv,
):
    f, w = lax.axis_index("feat"), lax.axis_index("width")
    member = lax.rem(f, group)
    base = f - member
    per = own.shape[0]
    rows = kept.shape[1]
    chunks = items // CHUNK

    barrier = pltpu.get_barrier_semaphore()
    for o in range(1, group):
        pl.semaphore_signal(barrier, 1, device_id=(base + lax.rem(member + o, group), w), device_id_type=MESH)
    for o in range(1, width):
        pl.semaphore_signal(barrier, 1, device_id=(f, lax.rem(w + o, width)), device_id_type=MESH)
    pl.semaphore_wait(barrier, group - 1 + width - 1)

    def group_copy(o, t):
        return pltpu.make_async_remote_copy(
            src_ref=own.at[t], dst_ref=table.at[member * per + t],
            send_sem=group_send.at[o - 1, t], recv_sem=group_recv.at[o - 1, t],
            device_id=(base + lax.rem(member + o, group), w), device_id_type=MESH,
        )

    def group_arrival(o, t):
        source = lax.rem(member + group - o, group)
        return pltpu.make_async_remote_copy(
            src_ref=own.at[t], dst_ref=table.at[source * per + t],
            send_sem=group_send.at[o - 1, t], recv_sem=group_recv.at[o - 1, t],
            device_id=(base + source, w), device_id_type=MESH,
        )

    for t in range(per):
        for o in range(1, group):
            group_copy(o, t).start()
    mine = pltpu.make_async_copy(own, table.at[pl.ds(member * per, per)], own_sem)
    mine.start()
    loads = [
        pltpu.make_async_copy(enc.at[t], targets.at[t], load_sem.at[t]) for t in range(enc.shape[0])
    ]
    for load in loads:
        load.start()
    for load in loads:
        load.wait()
    mine.wait()
    for t in range(per):
        for o in range(1, group):
            group_copy(o, t).wait_send()
            group_arrival(o, t).wait_recv()

    def share(o, c):
        peer = lax.rem(w + o, width)
        span = pl.ds(c * CHUNK, CHUNK)
        data = pltpu.make_async_remote_copy(
            src_ref=sent.at[o - 1, span], dst_ref=got.at[o - 1, span],
            send_sem=data_send.at[o - 1, c], recv_sem=data_recv.at[o - 1, c],
            device_id=(f, peer), device_id_type=MESH,
        )
        scale = pltpu.make_async_remote_copy(
            src_ref=sent_scale.at[o - 1, c], dst_ref=got_scale.at[o - 1, c],
            send_sem=scale_send.at[o - 1, c], recv_sem=scale_recv.at[o - 1, c],
            device_id=(f, peer), device_id_type=MESH,
        )
        return data, scale

    def send(c):
        for o in range(1, width):
            for copy in share(o, c):
                copy.start()

    def compute(c):
        def one(i, carry):
            n = c * CHUNK + i
            value = lax.dot_general(
                table[item_src[n]], targets[item_tile[n]], (((1,), (1,)), ((), ())),
                preferred_element_type=jnp.float32,
            )
            product[...] = value
            kept[n] = product[pl.ds(pl.multiple_of(w * rows, rows), rows), :]
            for o in range(1, width):
                peer = lax.rem(w + o, width)
                part = product[pl.ds(pl.multiple_of(peer * rows, rows), rows), :]
                peak = jnp.maximum(jnp.max(jnp.abs(part), axis=0, keepdims=True), 1e-30)
                sent[o - 1, n] = jnp.round(part * (TOP / peak)).astype(jnp.int32).astype(jnp.int16)
                sent_scale[o - 1, c, pl.ds(i, 1), :] = peak * (1.0 / TOP)
            return carry

        lax.fori_loop(0, CHUNK, one, 0)

    compute(0)

    def step(c, carry):
        compute(c)
        send(c - 1)
        return carry

    lax.fori_loop(1, chunks, step, 0)
    send(chunks - 1)

    def finish(c, carry):
        for o in range(1, width):
            for copy in share(o, c):
                copy.wait_recv()

        def one(i, carry):
            n = c * CHUNK + i
            total = kept[n]
            for o in range(1, width):
                total = total + got[o - 1, n].astype(jnp.int32).astype(jnp.float32) * got_scale[o - 1, c, pl.ds(i, 1), :]
            out[n] = (total * act[item_src[n]]).astype(out.dtype)
            return carry

        lax.fori_loop(0, CHUNK, one, 0)
        return carry

    lax.fori_loop(0, chunks, finish, 0)

    def drain(c, carry):
        for o in range(1, width):
            for copy in share(o, c):
                copy.wait_send()
        return carry

    lax.fori_loop(0, chunks, drain, 0)


def edges_of(items, slots, number, group, width, item_tile, item_src, act, own, enc):
    per, tile, depth = own.shape
    rows = tile // width
    chunks = items // CHUNK
    others = width - 1
    dma = pltpu.SemaphoreType.DMA
    smem = pl.BlockSpec(memory_space=pltpu.SMEM)
    vmem = pl.BlockSpec(memory_space=pltpu.VMEM)
    hbm = pl.BlockSpec(memory_space=pl.ANY)
    return pl.pallas_call(
        functools.partial(edge_kernel, items, group, width),
        out_shape=jax.ShapeDtypeStruct((slots, rows, tile), jnp.bfloat16),
        in_specs=[smem, smem, vmem, hbm, hbm],
        out_specs=vmem,
        scratch_shapes=[
            pltpu.VMEM((group * per, tile, depth), jnp.bfloat16),
            pltpu.VMEM(enc.shape, jnp.bfloat16),
            pltpu.VMEM((tile, tile), jnp.float32),
            pltpu.VMEM((items, rows, tile), jnp.float32),
            pltpu.VMEM((others, items, rows, tile), jnp.int16),
            pltpu.VMEM((others, chunks, CHUNK, tile), jnp.float32),
            pltpu.VMEM((others, items, rows, tile), jnp.int16),
            pltpu.VMEM((others, chunks, CHUNK, tile), jnp.float32),
            dma((enc.shape[0],)),
            dma,
            dma((max(group - 1, 1), per)),
            dma((max(group - 1, 1), per)),
            dma((others, chunks)),
            dma((others, chunks)),
            dma((others, chunks)),
            dma((others, chunks)),
        ],
        compiler_params=pltpu.CompilerParams(
            collective_id=number, has_side_effects=True, vmem_limit_bytes=60 * 2**20
        ),
        name=f"edges_{items}",
    )(item_tile, item_src, act, own, enc)


def place_kernel(place, counts, packed, out):
    t = pl.program_id(0)
    slots = out.shape[1]
    for k in range(slots):
        live = k < counts[t]

        @pl.when(live)
        def _():
            out[0, k] = packed[place[t * slots + k]]

        @pl.when(jnp.logical_not(live))
        def _():
            out[0, k] = jnp.zeros(out.shape[2:], out.dtype)


def place_tiles(place, counts, packed, targets, slots):
    rows, tile = packed.shape[1:]
    return pl.pallas_call(
        place_kernel,
        grid_spec=pltpu.PrefetchScalarGridSpec(
            num_scalar_prefetch=2,
            grid=(targets,),
            in_specs=[pl.BlockSpec(packed.shape, lambda t, *_: (0, 0, 0))],
            out_specs=pl.BlockSpec((1, slots, rows, tile), lambda t, *_: (t, 0, 0, 0)),
        ),
        out_shape=jax.ShapeDtypeStruct((targets, slots, rows, tile), packed.dtype),
        name="place_tiles",
    )(place, counts, packed)


def largest(value, axis):
    count = lax.axis_size(axis)
    apart = 1
    while apart < count:
        route = [(i, (i + apart) % count) for i in range(count)]
        value = jnp.maximum(value, lax.ppermute(value, axis, route))
        apart *= 2
    return value


def on_device(dec_rows, enc_rows, src_act, src_slots, counts, used_tiles):
    layers, used = used_tiles.shape
    group = lax.axis_size("feat") // layers
    width = lax.axis_size("width")
    device = lax.axis_index("feat")
    share = lax.axis_index("width")
    targets, maxs = src_slots.shape
    tile = enc_rows.shape[0] // targets
    depth = dec_rows.shape[1]
    members = dec_rows.shape[0] // tile
    per = used // group
    rows = tile // width
    member = device % group
    used_row = lax.dynamic_index_in_dim(used_tiles, device // group, 0, keepdims=False)
    own_ids = lax.dynamic_slice_in_dim(used_row, member * per, per) - member * members
    own = take_tiles(dec_rows.reshape(members, tile, depth), own_ids)
    enc = enc_rows.reshape(targets, tile, depth)
    act = src_act.reshape(-1, width, rows)[used_row]
    act = lax.dynamic_index_in_dim(act, share, 1, keepdims=False)
    act = jnp.broadcast_to(act[:, :, None], (used, rows, tile))

    slots = targets * maxs
    padded = -(-slots // CHUNK) * CHUNK
    index = jnp.arange(slots)
    live = (jnp.arange(maxs)[None, :] < counts[:, None]).reshape(-1)
    key = jnp.where(live, index, slots + index)
    place = jnp.sum((key[None, :] < key[:, None]).astype(jnp.int32), axis=1)
    packed_id = (jnp.arange(targets)[:, None] * used + src_slots).reshape(-1)
    hit = place[None, :] == jnp.arange(padded)[:, None]
    packed_id = jnp.sum(jnp.where(hit, packed_id[None, :], 0), axis=1)
    item_tile, item_src = packed_id // used, packed_id % used

    total = largest(jnp.sum(counts, keepdims=True), "feat")[0]
    sizes = sorted({-(-padded * part // (12 * CHUNK)) * CHUNK for part in (6, 7, 8, 9)} | {padded})
    choice = sum((total > size).astype(jnp.int32) for size in sizes[:-1])
    packed = lax.switch(
        choice,
        [functools.partial(edges_of, size, padded, i, group, width) for i, size in enumerate(sizes)],
        item_tile, item_src, act, own, enc,
    )
    return place_tiles(place, counts, packed, targets, maxs)


def solution(mesh):
    return jax.shard_map(
        on_device,
        mesh=mesh,
        in_specs=(P("feat", "width"), P("feat", "width"), P(), P("feat", None), P("feat"), P()),
        out_specs=P("feat", None, "width", None),
        check_vma=False,
    )
```

```python
import functools

import jax
import jax.numpy as jnp
from jax import lax
from jax.experimental import pallas as pl
from jax.experimental.pallas import tpu as pltpu
from jax.sharding import PartitionSpec as P

CHUNK = 8
TOP = 32767.0
MESH = pl.DeviceIdType.MESH


def take_kernel(ids, src, dst):
    dst[...] = src[...]


def take_tiles(tiles, ids):
    count = ids.shape[0]
    block = (1,) + tiles.shape[1:]
    return pl.pallas_call(
        take_kernel,
        grid_spec=pltpu.PrefetchScalarGridSpec(
            num_scalar_prefetch=1,
            grid=(count,),
            in_specs=[pl.BlockSpec(block, lambda i, ids: (ids[i], 0, 0))],
            out_specs=pl.BlockSpec(block, lambda i, ids: (i, 0, 0)),
        ),
        out_shape=jax.ShapeDtypeStruct((count,) + tiles.shape[1:], tiles.dtype),
        name="take_tiles",
    )(ids, tiles)


def edge_kernel(
    items, group, width,
    item_tile, item_src, act, own, enc, out,
    table, targets, product, kept, sent, sent_scale, got, got_scale,
    load_sem, own_sem, group_send, group_recv, data_send, data_recv, scale_send, scale_recv,
):
    f, w = lax.axis_index("feat"), lax.axis_index("width")
    member = lax.rem(f, group)
    base = f - member
    per = own.shape[0]
    rows = kept.shape[1]
    chunks = items // CHUNK

    barrier = pltpu.get_barrier_semaphore()
    for o in range(1, group):
        pl.semaphore_signal(barrier, 1, device_id=(base + lax.rem(member + o, group), w), device_id_type=MESH)
    for o in range(1, width):
        pl.semaphore_signal(barrier, 1, device_id=(f, lax.rem(w + o, width)), device_id_type=MESH)
    pl.semaphore_wait(barrier, group - 1 + width - 1)

    def group_copy(o, t):
        return pltpu.make_async_remote_copy(
            src_ref=own.at[t], dst_ref=table.at[member * per + t],
            send_sem=group_send.at[o - 1, t], recv_sem=group_recv.at[o - 1, t],
            device_id=(base + lax.rem(member + o, group), w), device_id_type=MESH,
        )

    def group_arrival(o, t):
        source = lax.rem(member + group - o, group)
        return pltpu.make_async_remote_copy(
            src_ref=own.at[t], dst_ref=table.at[source * per + t],
            send_sem=group_send.at[o - 1, t], recv_sem=group_recv.at[o - 1, t],
            device_id=(base + source, w), device_id_type=MESH,
        )

    for t in range(per):
        for o in range(1, group):
            group_copy(o, t).start()
    mine = pltpu.make_async_copy(own, table.at[pl.ds(member * per, per)], own_sem)
    mine.start()
    loads = [
        pltpu.make_async_copy(enc.at[t], targets.at[t], load_sem.at[t]) for t in range(enc.shape[0])
    ]
    for load in loads:
        load.start()
    for load in loads:
        load.wait()
    mine.wait()
    for t in range(per):
        for o in range(1, group):
            group_copy(o, t).wait_send()
            group_arrival(o, t).wait_recv()

    def share(o, c):
        peer = lax.rem(w + o, width)
        span = pl.ds(c * CHUNK, CHUNK)
        data = pltpu.make_async_remote_copy(
            src_ref=sent.at[o - 1, span], dst_ref=got.at[o - 1, span],
            send_sem=data_send.at[o - 1, c], recv_sem=data_recv.at[o - 1, c],
            device_id=(f, peer), device_id_type=MESH,
        )
        scale = pltpu.make_async_remote_copy(
            src_ref=sent_scale.at[o - 1, c], dst_ref=got_scale.at[o - 1, c],
            send_sem=scale_send.at[o - 1, c], recv_sem=scale_recv.at[o - 1, c],
            device_id=(f, peer), device_id_type=MESH,
        )
        return data, scale

    def send(c):
        for o in range(1, width):
            for copy in share(o, c):
                copy.start()

    def compute(c):
        def one(i, carry):
            n = c * CHUNK + i
            value = lax.dot_general(
                table[item_src[n]], targets[item_tile[n]], (((1,), (1,)), ((), ())),
                preferred_element_type=jnp.float32,
            )
            product[...] = value
            kept[n] = product[pl.ds(pl.multiple_of(w * rows, rows), rows), :]
            for o in range(1, width):
                peer = lax.rem(w + o, width)
                part = product[pl.ds(pl.multiple_of(peer * rows, rows), rows), :]
                peak = jnp.maximum(jnp.max(jnp.abs(part), axis=0, keepdims=True), 1e-30)
                sent[o - 1, n] = jnp.round(part * (TOP / peak)).astype(jnp.int32).astype(jnp.int16)
                sent_scale[o - 1, c, pl.ds(i, 1), :] = peak * (1.0 / TOP)
            return carry

        lax.fori_loop(0, CHUNK, one, 0)

    compute(0)

    def step(c, carry):
        compute(c)
        send(c - 1)
        return carry

    lax.fori_loop(1, chunks, step, 0)
    send(chunks - 1)

    def finish(c, carry):
        for o in range(1, width):
            for copy in share(o, c):
                copy.wait_recv()

        def one(i, carry):
            n = c * CHUNK + i
            total = kept[n]
            for o in range(1, width):
                total = total + got[o - 1, n].astype(jnp.int32).astype(jnp.float32) * got_scale[o - 1, c, pl.ds(i, 1), :]
            out[n] = (total * act[item_src[n]]).astype(out.dtype)
            return carry

        lax.fori_loop(0, CHUNK, one, 0)
        return carry

    lax.fori_loop(0, chunks, finish, 0)

    def drain(c, carry):
        for o in range(1, width):
            for copy in share(o, c):
                copy.wait_send()
        return carry

    lax.fori_loop(0, chunks, drain, 0)


def edges_of(items, slots, number, group, width, item_tile, item_src, act, own, enc):
    per, tile, depth = own.shape
    rows = tile // width
    chunks = items // CHUNK
    others = width - 1
    dma = pltpu.SemaphoreType.DMA
    smem = pl.BlockSpec(memory_space=pltpu.SMEM)
    vmem = pl.BlockSpec(memory_space=pltpu.VMEM)
    hbm = pl.BlockSpec(memory_space=pl.ANY)
    return pl.pallas_call(
        functools.partial(edge_kernel, items, group, width),
        out_shape=jax.ShapeDtypeStruct((slots, rows, tile), jnp.bfloat16),
        in_specs=[smem, smem, vmem, hbm, hbm],
        out_specs=vmem,
        scratch_shapes=[
            pltpu.VMEM((group * per, tile, depth), jnp.bfloat16),
            pltpu.VMEM(enc.shape, jnp.bfloat16),
            pltpu.VMEM((tile, tile), jnp.float32),
            pltpu.VMEM((items, rows, tile), jnp.float32),
            pltpu.VMEM((others, items, rows, tile), jnp.int16),
            pltpu.VMEM((others, chunks, CHUNK, tile), jnp.float32),
            pltpu.VMEM((others, items, rows, tile), jnp.int16),
            pltpu.VMEM((others, chunks, CHUNK, tile), jnp.float32),
            dma((enc.shape[0],)),
            dma,
            dma((max(group - 1, 1), per)),
            dma((max(group - 1, 1), per)),
            dma((others, chunks)),
            dma((others, chunks)),
            dma((others, chunks)),
            dma((others, chunks)),
        ],
        compiler_params=pltpu.CompilerParams(
            collective_id=number, has_side_effects=True, vmem_limit_bytes=60 * 2**20
        ),
        name=f"edges_{items}",
    )(item_tile, item_src, act, own, enc)


def place_kernel(place, counts, packed, out):
    t = pl.program_id(0)
    slots = out.shape[1]
    for k in range(slots):
        value = packed[place[t * slots + k]]
        out[0, k] = jnp.where(k < counts[t], value, jnp.zeros_like(value))


def place_tiles(place, counts, packed, targets, slots):
    rows, tile = packed.shape[1:]
    return pl.pallas_call(
        place_kernel,
        grid_spec=pltpu.PrefetchScalarGridSpec(
            num_scalar_prefetch=2,
            grid=(targets,),
            in_specs=[pl.BlockSpec(packed.shape, lambda t, *_: (0, 0, 0))],
            out_specs=pl.BlockSpec((1, slots, rows, tile), lambda t, *_: (t, 0, 0, 0)),
        ),
        out_shape=jax.ShapeDtypeStruct((targets, slots, rows, tile), packed.dtype),
        name="place_tiles",
    )(place, counts, packed)


def largest_kernel(count, value, out, seen, own_sem, send_sem, recv_sem):
    f, w = lax.axis_index("feat"), lax.axis_index("width")
    barrier = pltpu.get_barrier_semaphore()

    def peer(o):
        return (lax.rem(f + o, count), w)

    def greet(o, carry):
        pl.semaphore_signal(barrier, 1, device_id=peer(o), device_id_type=MESH)
        return carry

    lax.fori_loop(1, count, greet, 0)
    mine = pltpu.make_async_copy(value, seen.at[0], own_sem)
    mine.start()
    pl.semaphore_wait(barrier, count - 1)

    def copy(o):
        return pltpu.make_async_remote_copy(
            src_ref=value, dst_ref=seen.at[o], send_sem=send_sem.at[o], recv_sem=recv_sem.at[o],
            device_id=peer(o), device_id_type=MESH,
        )

    def start(o, carry):
        copy(o).start()
        return carry

    def finish(o, carry):
        copy(o).wait()
        return carry

    lax.fori_loop(1, count, start, 0)
    mine.wait()
    lax.fori_loop(1, count, finish, 0)
    out[...] = jnp.max(seen[...], axis=0)


def largest(value, number):
    count = lax.axis_size("feat")
    shape = (8, 128)
    dma = pltpu.SemaphoreType.DMA
    vmem = pl.BlockSpec(memory_space=pltpu.VMEM)
    return pl.pallas_call(
        functools.partial(largest_kernel, count),
        out_shape=jax.ShapeDtypeStruct(shape, jnp.int32),
        in_specs=[vmem],
        out_specs=vmem,
        scratch_shapes=[pltpu.VMEM((count,) + shape, jnp.int32), dma, dma((count,)), dma((count,))],
        compiler_params=pltpu.CompilerParams(
            collective_id=number, has_side_effects=True, vmem_limit_bytes=2**20
        ),
        name="largest",
    )(jnp.broadcast_to(value, shape))[0, 0]


def on_device(dec_rows, enc_rows, src_act, src_slots, counts, used_tiles):
    layers, used = used_tiles.shape
    group = lax.axis_size("feat") // layers
    width = lax.axis_size("width")
    device = lax.axis_index("feat")
    share = lax.axis_index("width")
    targets, maxs = src_slots.shape
    tile = enc_rows.shape[0] // targets
    depth = dec_rows.shape[1]
    members = dec_rows.shape[0] // tile
    per = used // group
    rows = tile // width
    member = device % group
    used_row = lax.dynamic_index_in_dim(used_tiles, device // group, 0, keepdims=False)
    own_ids = lax.dynamic_slice_in_dim(used_row, member * per, per) - member * members
    own = take_tiles(dec_rows.reshape(members, tile, depth), own_ids)
    enc = enc_rows.reshape(targets, tile, depth)
    act = src_act.reshape(-1, width, rows)[used_row]
    act = lax.dynamic_index_in_dim(act, share, 1, keepdims=False)
    act = jnp.broadcast_to(act[:, :, None], (used, rows, tile))

    slots = targets * maxs
    padded = -(-slots // CHUNK) * CHUNK
    index = jnp.arange(slots)
    live = (jnp.arange(maxs)[None, :] < counts[:, None]).reshape(-1)
    key = jnp.where(live, index, slots + index)
    place = jnp.sum((key[None, :] < key[:, None]).astype(jnp.int32), axis=1)
    packed_id = (jnp.arange(targets)[:, None] * used + src_slots).reshape(-1)
    hit = place[None, :] == jnp.arange(padded)[:, None]
    packed_id = jnp.sum(jnp.where(hit, packed_id[None, :], 0), axis=1)
    item_tile, item_src = packed_id // used, packed_id % used

    sizes = sorted({-(-padded * part // (24 * CHUNK)) * CHUNK for part in range(12, 19)} | {padded})
    total = largest(jnp.sum(counts), len(sizes))
    choice = sum((total > size).astype(jnp.int32) for size in sizes[:-1])
    packed = lax.switch(
        choice,
        [functools.partial(edges_of, size, padded, i, group, width) for i, size in enumerate(sizes)],
        item_tile, item_src, act, own, enc,
    )
    return place_tiles(place, counts, packed, targets, maxs)


def solution(mesh):
    return jax.shard_map(
        on_device,
        mesh=mesh,
        in_specs=(P("feat", "width"), P("feat", "width"), P(), P("feat", None), P("feat"), P()),
        out_specs=P("feat", None, "width", None),
        check_vma=False,
    )
```
